1024 devices in a mesh: dp: 16 (over x_lo, y, core), mp: 32 (over z), pipe: 2 (over x_hi).
Axes of the slice: x: 4 (x_hi: 2, x_lo: 2; x = x_hi * 2 + x_lo), y: 4, z: 32, core: 2. Of those that a mesh axis runs over, the one named last changes fastest.
Arguments:
- activations: bfloat16 [32768, 4096], P(('dp', 'pipe')), may hold values from -6 to 6
- cotangent: bfloat16 [32768, 11008], P(('dp', 'pipe'), 'mp'), may hold values from -0.03125 to 0.03125
- projection_basis: bfloat16 [4096, 1024], P(None, 'mp'), may hold values from -0.09375 to 0.09375
- first_moment: float32 [1024, 11008], P(('dp', 'pipe'), 'mp'), may hold values from -4 to 4
- second_moment: float32 [1024, 11008], P(('dp', 'pipe'), 'mp'), may hold values from 0.25 to 4
Outputs:
- update: float32 [4096, 11008], P(('dp', 'pipe'), 'mp')
- first_new: float32 [1024, 11008], P(('dp', 'pipe'), 'mp')
- second_new: float32 [1024, 11008], P(('dp', 'pipe'), 'mp')
The draws below stay inside these ranges and needn't reach their ends.
All inputs are finite; a program needn't handle non-finite values.
Results may differ from the reference program's by a relative error of at most 0.0031.
Values may be sent and summed in bfloat16 or wider, within the bound.
No kernel may reach another device: no remote copies, remote signals or barrier semaphores. Data moves between devices by JAX's collectives and lax.ppermute only.
A program may use at most 32 MiB of HBM per device.

```python
import math
import jax
import jax.numpy as jnp
from jax import lax

D = 4096
FF = 11008
R = 1024
TOKENS = 32768


def block_levels(key, extent, shards, low, high):
    gain, own = 1.0, jax.random.fold_in(key, 6)
    for axis_at, parts in shards:
        heights = jnp.exp(jax.random.uniform(jax.random.fold_in(own, axis_at), (parts,), jnp.float32, low / len(shards), high / len(shards)))
        gain = gain * jnp.repeat(heights, extent[axis_at] // parts).reshape([-1 if axis == axis_at else 1 for axis in range(len(extent))])
    return gain


def normal_values(stream_key, shape, scale, limit, pieces=(), held_as=jnp.bfloat16):
    array = scale * jax.random.normal(stream_key, shape, jnp.float32)
    if pieces:
        array = array * block_levels(stream_key, shape, pieces, -0.22, 0.18)
    return jnp.clip(array, -limit, limit).astype(held_as)


def setup_inputs(seed: int = 0) -> dict:
    splits = jax.random.split(jax.random.key(seed), 6)
    activations = normal_values(splits[0], (TOKENS, D), 1.0, 6.0, ((0, 32),))
    cotangent = normal_values(splits[1], (TOKENS, FF), TOKENS ** -0.5, 0.03125, ((0, 32), (1, 32)))
    projection_basis = normal_values(splits[2], (D, R), D ** -0.5, 0.09375, ((1, 32),))
    first_moment = normal_values(splits[3], (R, FF), 0.3, 4.0, ((0, 32), (1, 32)), jnp.float32)
    second_moment = jnp.clip(jnp.exp(math.log(4.0) - 2.7725887 * jax.random.uniform(splits[4], (R, FF), jnp.float32) ** block_levels(splits[4], (R, FF), ((0, 32), (1, 32)), -0.2, 0.2)), 0.25, 4.0)
    return {"activations": activations, "cotangent": cotangent, "projection_basis": projection_basis, "first_moment": first_moment, "second_moment": second_moment}


beta_first = 0.9
beta_second = 0.999
correction_first = 1.0
correction_second = 0.632304575
epsilon = 1e-08
galore_scale = 0.25

def reference(activations, cotangent, projection_basis, first_moment, second_moment):
    projected = jnp.dot(activations, projection_basis, preferred_element_type=jnp.float32).astype(jnp.bfloat16)
    gradient = lax.dot_general(projected, cotangent, (((0,), (0,)), ((), ())), preferred_element_type=jnp.float32)
    first_new = beta_first * first_moment + (1.0 - beta_first) * gradient
    second_new = beta_second * second_moment + (1.0 - beta_second) * gradient * gradient
    direction = (first_new / correction_first / (jnp.sqrt(second_new / correction_second) + epsilon)).astype(jnp.bfloat16)
    update = galore_scale * jnp.dot(projection_basis, direction, preferred_element_type=jnp.float32)
    return (update, first_new, second_new)
```

```python
import jax
import jax.numpy as jnp
from jax import lax
from jax.sharding import PartitionSpec as P

beta_first = 0.9
beta_second = 0.999
correction_first = 1.0
correction_second = 0.632304575
epsilon = 1e-08
galore_scale = 0.25

DATA = ("dp", "pipe")


def spread(x, axes, n):
    return lax.all_to_all(jnp.broadcast_to(x[None], (n, *x.shape)), axes, 0, 0)


def on_device(activations, cotangent, projection_basis, first_moment, second_moment):
    n_data, n_mp = lax.axis_size(DATA), lax.axis_size("mp")
    here = lax.axis_index(DATA)
    width, own_rank = projection_basis.shape
    rows, tile_rows, hidden = width // n_data, first_moment.shape[0], cotangent.shape[1]
    own_rows = lax.dynamic_slice_in_dim(projection_basis, here * rows, rows, 0).T
    basis_rows = spread(own_rows, "mp", n_mp).reshape(n_mp * own_rank, rows)
    whole_grad = lax.dot_general(
        activations, cotangent, (((0,), (0,)), ((), ())), preferred_element_type=jnp.float32
    ).astype(jnp.bfloat16)
    pieces = lax.all_to_all(whole_grad.reshape(n_data, rows, hidden), DATA, 0, 0)
    grad_rows = jnp.sum(pieces.astype(jnp.float32), axis=0)
    high = grad_rows.astype(jnp.bfloat16)
    low = (grad_rows - high.astype(jnp.float32)).astype(jnp.bfloat16)
    partial_grad = (
        jnp.dot(basis_rows, high, preferred_element_type=jnp.float32)
        + jnp.dot(basis_rows, low, preferred_element_type=jnp.float32)
    ).astype(jnp.bfloat16)
    tiles = lax.all_to_all(partial_grad.reshape(n_data, tile_rows, hidden), DATA, 0, 0)
    grad_tile = jnp.sum(tiles.astype(jnp.float32), axis=0)
    first_new = beta_first * first_moment + (1.0 - beta_first) * grad_tile
    second_new = beta_second * second_moment + (1.0 - beta_second) * grad_tile * grad_tile
    direction = (
        first_new / correction_first / (jnp.sqrt(second_new / correction_second) + epsilon)
    ).astype(jnp.bfloat16)
    directions = spread(direction, DATA, n_data).reshape(n_data * tile_rows, hidden)
    folded = lax.dot_general(
        basis_rows, directions, (((0,), (0,)), ((), ())), preferred_element_type=jnp.float32
    )
    return (galore_scale * folded, first_new, second_new)


def solution(mesh):
    return jax.shard_map(
        on_device,
        mesh=mesh,
        in_specs=(
            P(DATA, None),
            P(DATA, "mp"),
            P(None, "mp"),
            P(DATA, "mp"),
            P(DATA, "mp"),
        ),
        out_specs=(P(DATA, "mp"), P(DATA, "mp"), P(DATA, "mp")),
        check_vma=False,
    )
```

```python
import jax
import jax.numpy as jnp
from jax import lax
from jax.experimental import pallas as pl
from jax.experimental.pallas import tpu as pltpu
from jax.sharding import Mesh, PartitionSpec as P

beta_first = 0.9
beta_second = 0.999
correction_first = 1.0
correction_second = 0.632304575
epsilon = 1e-08
galore_scale = 0.25

DATA = ("xl", "y", "core", "xh")
MP = ("far", "near")


def spread(x, axes):
    n = lax.axis_size(axes)
    return lax.all_to_all(jnp.broadcast_to(x[None], (n, *x.shape)), axes, 0, 0)


def grad_kernel(cot_ref, act_ref, out_ref):
    block = jnp.dot(cot_ref[...], act_ref[...], preferred_element_type=jnp.float32)
    width = out_ref.shape[2]
    for piece in range(out_ref.shape[0]):
        out_ref[piece] = block[:, piece * width : (piece + 1) * width].astype(out_ref.dtype)


def whole_grad(cotangent, activations, pieces, per_step=2):
    tokens, width = activations.shape
    hidden = cotangent.shape[0]
    cols = width // pieces
    return pl.pallas_call(
        grad_kernel,
        grid=(pieces // per_step,),
        in_specs=[
            pl.BlockSpec((hidden, tokens), lambda i: (0, 0)),
            pl.BlockSpec((tokens, per_step * cols), lambda i: (0, i)),
        ],
        out_specs=pl.BlockSpec((per_step, hidden, cols), lambda i: (i, 0, 0)),
        out_shape=jax.ShapeDtypeStruct((pieces, hidden, cols), jnp.bfloat16),
        compiler_params=pltpu.CompilerParams(vmem_limit_bytes=32 << 20),
        name="whole_grad",
    )(cotangent, activations)


def on_device(activations, cotangent, projection_basis, first_moment, second_moment):
    n_data = lax.axis_size(DATA)
    here = lax.axis_index(DATA)
    width, own_rank = projection_basis.shape
    rows, tile_rows, hidden = width // n_data, first_moment.shape[0], cotangent.shape[1]

    own_rows = lax.dynamic_slice_in_dim(projection_basis.T, here * rows, rows, 1)
    near_rows = spread(own_rows, "near")
    pieces = whole_grad(cotangent.T, activations, n_data)
    pieces, near_rows = lax.optimization_barrier((pieces, near_rows))
    basis_rows = lax.all_gather(near_rows, "far", axis=0).reshape(-1, rows)

    pieces = lax.all_to_all(pieces, DATA, 0, 0)
    grad_rows = jnp.sum(pieces.astype(jnp.float32), axis=0)
    high = grad_rows.astype(jnp.bfloat16)
    low = (grad_rows - high.astype(jnp.float32)).astype(jnp.bfloat16)
    partial_grad = jnp.dot(
        jnp.concatenate([basis_rows, basis_rows], axis=1),
        jnp.concatenate([high, low], axis=1).T,
        preferred_element_type=jnp.float32,
    ).astype(jnp.bfloat16)
    tiles = lax.all_to_all(partial_grad.reshape(n_data, tile_rows, hidden), DATA, 0, 0)
    grad_tile = jnp.sum(tiles.astype(jnp.float32), axis=0)
    first_new = beta_first * first_moment + (1.0 - beta_first) * grad_tile
    second_new = beta_second * second_moment + (1.0 - beta_second) * grad_tile * grad_tile
    direction = (
        first_new / correction_first / (jnp.sqrt(second_new / correction_second) + epsilon)
    ).astype(jnp.bfloat16)
    directions = spread(direction, DATA).reshape(n_data * tile_rows, hidden)
    folded = lax.dot_general(
        basis_rows, directions, (((0,), (0,)), ((), ())), preferred_element_type=jnp.float32
    )
    return (galore_scale * folded, first_new, second_new)


def solution(mesh):
    dp, mp, pipe = mesh.devices.shape
    fine = Mesh(
        mesh.devices.reshape(2, dp // 4, 2, 4, mp // 4, pipe),
        ("xl", "y", "core", "far", "near", "xh"),
    )
    return jax.shard_map(
        on_device,
        mesh=fine,
        in_specs=(
            P(DATA, None),
            P(DATA, MP),
            P(None, MP),
            P(DATA, MP),
            P(DATA, MP),
        ),
        out_specs=(P(DATA, MP), P(DATA, MP), P(DATA, MP)),
        check_vma=False,
    )
```

```python
import jax
import jax.numpy as jnp
from jax import lax
from jax.experimental import pallas as pl
from jax.experimental.pallas import tpu as pltpu
from jax.sharding import Mesh, PartitionSpec as P

beta_first = 0.9
beta_second = 0.999
correction_first = 1.0
correction_second = 0.632304575
epsilon = 1e-08
galore_scale = 0.25

DATA = ("xl", "y", "core", "xh")
MP = ("far", "near")


def spread(x, axes):
    n = lax.axis_size(axes)
    return lax.all_to_all(jnp.broadcast_to(x[None], (n, *x.shape)), axes, 0, 0)


def grad_kernel(cot_hbm, act_hbm, out_hbm, cot, act, out, cot_sem, in_sem, out_sem):
    chunks, per_chunk, width = out.shape[0], out.shape[1], out.shape[3]
    cols = per_chunk * width

    def fetch(c):
        return pltpu.make_async_copy(
            act_hbm.at[:, c * cols : (c + 1) * cols], act.at[c], in_sem.at[c]
        )

    def send(c):
        return pltpu.make_async_copy(
            out.at[c], out_hbm.at[c * per_chunk : (c + 1) * per_chunk], out_sem.at[c]
        )

    whole = pltpu.make_async_copy(cot_hbm, cot, cot_sem)
    whole.start()
    for c in range(chunks):
        fetch(c).start()
    whole.wait()
    for c in range(chunks):
        fetch(c).wait()
        block = jnp.dot(cot[...], act[c], preferred_element_type=jnp.float32)
        for p in range(per_chunk):
            out[c, p] = block[:, p * width : (p + 1) * width].astype(out.dtype)
        send(c).start()
    for c in range(chunks):
        send(c).wait()


def whole_grad(cotangent, activations, pieces, chunks=2):
    tokens, width = activations.shape
    hidden, cols = cotangent.shape[0], width // pieces
    per_chunk = pieces // chunks
    return pl.pallas_call(
        grad_kernel,
        in_specs=[
            pl.BlockSpec(memory_space=pltpu.HBM),
            pl.BlockSpec(memory_space=pltpu.HBM),
        ],
        out_specs=pl.BlockSpec(memory_space=pltpu.HBM),
        out_shape=jax.ShapeDtypeStruct((pieces, hidden, cols), jnp.bfloat16),
        scratch_shapes=[
            pltpu.VMEM(cotangent.shape, cotangent.dtype),
            pltpu.VMEM((chunks, tokens, per_chunk * cols), jnp.bfloat16),
            pltpu.VMEM((chunks, per_chunk, hidden, cols), jnp.bfloat16),
            pltpu.SemaphoreType.DMA,
            pltpu.SemaphoreType.DMA((chunks,)),
            pltpu.SemaphoreType.DMA((chunks,)),
        ],
        compiler_params=pltpu.CompilerParams(vmem_limit_bytes=40 << 20),
        name="whole_grad",
    )(
        pltpu.with_memory_space_constraint(cotangent, pltpu.HBM),
        pltpu.with_memory_space_constraint(activations, pltpu.HBM),
    )


def on_device(activations, cotangent, projection_basis, first_moment, second_moment):
    n_data = lax.axis_size(DATA)
    here = lax.axis_index(DATA)
    width, own_rank = projection_basis.shape
    rows, tile_rows, hidden = width // n_data, first_moment.shape[0], cotangent.shape[1]

    own_rows = lax.dynamic_slice_in_dim(projection_basis.T, here * rows, rows, 1)
    near_rows = spread(own_rows, "near")
    pieces = whole_grad(cotangent.T, activations, n_data)
    pieces, near_rows = lax.optimization_barrier((pieces, near_rows))
    basis_rows = lax.all_gather(near_rows, "far", axis=0).reshape(-1, rows)

    pieces = lax.all_to_all(pieces, DATA, 0, 0)
    grad_rows = jnp.sum(pieces.astype(jnp.float32), axis=0)
    high = grad_rows.astype(jnp.bfloat16)
    low = (grad_rows - high.astype(jnp.float32)).astype(jnp.bfloat16)
    partial_grad = jnp.dot(
        jnp.concatenate([basis_rows, basis_rows], axis=1),
        jnp.concatenate([high, low], axis=1).T,
        preferred_element_type=jnp.float32,
    ).astype(jnp.bfloat16)
    tiles = lax.all_to_all(partial_grad.reshape(n_data, tile_rows, hidden), DATA, 0, 0)
    grad_tile = jnp.sum(tiles.astype(jnp.float32), axis=0)
    first_new = beta_first * first_moment + (1.0 - beta_first) * grad_tile
    second_new = beta_second * second_moment + (1.0 - beta_second) * grad_tile * grad_tile
    direction = (
        first_new / correction_first / (jnp.sqrt(second_new / correction_second) + epsilon)
    ).astype(jnp.bfloat16)
    directions = spread(direction, DATA).reshape(n_data * tile_rows, hidden)
    folded = lax.dot_general(
        basis_rows, directions, (((0,), (0,)), ((), ())), preferred_element_type=jnp.float32
    )
    return (galore_scale * folded, first_new, second_new)


def solution(mesh):
    dp, mp, pipe = mesh.devices.shape
    fine = Mesh(
        mesh.devices.reshape(2, dp // 4, 2, 4, mp // 4, pipe),
        ("xl", "y", "core", "far", "near", "xh"),
    )
    return jax.shard_map(
        on_device,
        mesh=fine,
        in_specs=(
            P(DATA, None),
            P(DATA, MP),
            P(None, MP),
            P(DATA, MP),
            P(DATA, MP),
        ),
        out_specs=(P(DATA, MP), P(DATA, MP), P(DATA, MP)),
        check_vma=False,
    )
```

```python
import jax
import jax.numpy as jnp
from jax import lax
from jax.experimental import pallas as pl
from jax.experimental.pallas import tpu as pltpu
from jax.sharding import Mesh, PartitionSpec as P

beta_first = 0.9
beta_second = 0.999
correction_first = 1.0
correction_second = 0.632304575
epsilon = 1e-08
galore_scale = 0.25

DATA = ("xl", "y", "core", "xh")
CHIPS = ("xl", "y", "xh")
MP = ("far", "near")


def spread(x, axes):
    n = lax.axis_size(axes)
    return lax.all_to_all(jnp.broadcast_to(x[None], (n, *x.shape)), axes, 0, 0)


def grad_kernel(cot_hbm, act_hbm, out_hbm, cot, act, out, cot_sem, in_sem, out_sem):
    chunks, per_chunk, width = out.shape[0], out.shape[1], out.shape[3]
    cols = per_chunk * width

    def fetch(c):
        return pltpu.make_async_copy(
            act_hbm.at[:, c * cols : (c + 1) * cols], act.at[c], in_sem.at[c]
        )

    def send(c):
        return pltpu.make_async_copy(
            out.at[c], out_hbm.at[c * per_chunk : (c + 1) * per_chunk], out_sem.at[c]
        )

    whole = pltpu.make_async_copy(cot_hbm, cot, cot_sem)
    whole.start()
    for c in range(chunks):
        fetch(c).start()
    whole.wait()
    for c in range(chunks):
        fetch(c).wait()
        block = jnp.dot(cot[...], act[c], preferred_element_type=jnp.float32)
        for p in range(per_chunk):
            out[c, p] = block[:, p * width : (p + 1) * width].astype(out.dtype)
        send(c).start()
    for c in range(chunks):
        send(c).wait()


def whole_grad(cotangent, activations, pieces, chunks=2):
    tokens, width = activations.shape
    hidden, cols = cotangent.shape[0], width // pieces
    per_chunk = pieces // chunks
    return pl.pallas_call(
        grad_kernel,
        in_specs=[
            pl.BlockSpec(memory_space=pltpu.HBM),
            pl.BlockSpec(memory_space=pltpu.HBM),
        ],
        out_specs=pl.BlockSpec(memory_space=pltpu.HBM),
        out_shape=jax.ShapeDtypeStruct((pieces, hidden, cols), jnp.bfloat16),
        scratch_shapes=[
            pltpu.VMEM(cotangent.shape, cotangent.dtype),
            pltpu.VMEM((chunks, tokens, per_chunk * cols), jnp.bfloat16),
            pltpu.VMEM((chunks, per_chunk, hidden, cols), jnp.bfloat16),
            pltpu.SemaphoreType.DMA,
            pltpu.SemaphoreType.DMA((chunks,)),
            pltpu.SemaphoreType.DMA((chunks,)),
        ],
        compiler_params=pltpu.CompilerParams(vmem_limit_bytes=40 << 20),
        name="whole_grad",
    )(
        pltpu.with_memory_space_constraint(cotangent, pltpu.HBM),
        pltpu.with_memory_space_constraint(activations, pltpu.HBM),
    )


def on_device(activations, cotangent, projection_basis, first_moment, second_moment):
    n_data = lax.axis_size(DATA)
    here = lax.axis_index(DATA)
    width, own_rank = projection_basis.shape
    rows, tile_rows, hidden = width // n_data, first_moment.shape[0], cotangent.shape[1]

    own_rows = lax.dynamic_slice_in_dim(projection_basis.T, here * rows, rows, 1)
    near_rows = spread(own_rows, "near")
    pieces = whole_grad(cotangent.T, activations, n_data)
    pieces, near_rows = lax.optimization_barrier((pieces, near_rows))
    basis_rows = lax.all_gather(near_rows, "far", axis=0).reshape(-1, rows)

    pieces = lax.all_to_all(pieces, DATA, 0, 0)
    grad_rows = jnp.sum(pieces.astype(jnp.float32), axis=0)
    high = grad_rows.astype(jnp.bfloat16)
    low = (grad_rows - high.astype(jnp.float32)).astype(jnp.bfloat16)
    partial_grad = jnp.dot(
        jnp.concatenate([basis_rows, basis_rows], axis=1),
        jnp.concatenate([high, low], axis=1).T,
        preferred_element_type=jnp.float32,
    ).astype(jnp.bfloat16)
    tiles = lax.all_to_all(partial_grad.reshape(n_data, tile_rows, hidden), DATA, 0, 0)
    grad_tile = jnp.sum(tiles.astype(jnp.float32), axis=0)
    first_new = beta_first * first_moment + (1.0 - beta_first) * grad_tile
    second_new = beta_second * second_moment + (1.0 - beta_second) * grad_tile * grad_tile
    direction = (
        first_new / correction_first / (jnp.sqrt(second_new / correction_second) + epsilon)
    ).astype(jnp.bfloat16)
    directions = lax.all_gather(spread(direction, CHIPS), "core", axis=0)
    directions = directions.reshape(2, -1, 2, tile_rows, hidden).transpose(1, 0, 2, 3, 4)
    directions = directions.reshape(n_data * tile_rows, hidden)
    folded = lax.dot_general(
        basis_rows, directions, (((0,), (0,)), ((), ())), preferred_element_type=jnp.float32
    )
    return (galore_scale * folded, first_new, second_new)


def solution(mesh):
    dp, mp, pipe = mesh.devices.shape
    fine = Mesh(
        mesh.devices.reshape(2, dp // 4, 2, mp // 4, 4, pipe),
        ("xl", "y", "core", "far", "near", "xh"),
    )
    return jax.shard_map(
        on_device,
        mesh=fine,
        in_specs=(
            P(DATA, None),
            P(DATA, MP),
            P(None, MP),
            P(DATA, MP),
            P(DATA, MP),
        ),
        out_specs=(P(DATA, MP), P(DATA, MP), P(DATA, MP)),
        check_vma=False,
    )
```

```python
import jax
import jax.numpy as jnp
from jax import lax
from jax.experimental import pallas as pl
from jax.experimental.pallas import tpu as pltpu
from jax.sharding import Mesh, PartitionSpec as P

beta_first = 0.9
beta_second = 0.999
correction_first = 1.0
correction_second = 0.632304575
epsilon = 1e-08
galore_scale = 0.25

DATA = ("xl", "y", "core", "xh")
CHIPS = ("xl", "y", "xh")
MP = ("far", "near")


def spread(x, axes):
    n = lax.axis_size(axes)
    return lax.all_to_all(jnp.broadcast_to(x[None], (n, *x.shape)), axes, 0, 0)


def grad_kernel(cot_hbm, act_hbm, out_hbm, cot, act, out, cot_sem, in_sem, out_sem):
    chunks, per_chunk, width = out.shape[0], out.shape[1], out.shape[3]
    cols = per_chunk * width

    def fetch(c):
        return pltpu.make_async_copy(
            act_hbm.at[:, c * cols : (c + 1) * cols], act.at[c], in_sem.at[c]
        )

    def send(c):
        return pltpu.make_async_copy(
            out.at[c], out_hbm.at[c * per_chunk : (c + 1) * per_chunk], out_sem.at[c]
        )

    whole = pltpu.make_async_copy(cot_hbm, cot, cot_sem)
    whole.start()
    for c in range(chunks):
        fetch(c).start()
    whole.wait()
    for c in range(chunks):
        fetch(c).wait()
        block = jnp.dot(cot[...], act[c], preferred_element_type=jnp.float32)
        for p in range(per_chunk):
            out[c, p] = block[:, p * width : (p + 1) * width].astype(out.dtype)
        send(c).start()
    for c in range(chunks):
        send(c).wait()


def whole_grad(cotangent, activations, pieces, chunks=2):
    tokens, width = activations.shape
    hidden, cols = cotangent.shape[0], width // pieces
    per_chunk = pieces // chunks
    return pl.pallas_call(
        grad_kernel,
        in_specs=[
            pl.BlockSpec(memory_space=pltpu.HBM),
            pl.BlockSpec(memory_space=pltpu.HBM),
        ],
        out_specs=pl.BlockSpec(memory_space=pltpu.HBM),
        out_shape=jax.ShapeDtypeStruct((pieces, hidden, cols), jnp.bfloat16),
        scratch_shapes=[
            pltpu.VMEM(cotangent.shape, cotangent.dtype),
            pltpu.VMEM((chunks, tokens, per_chunk * cols), jnp.bfloat16),
            pltpu.VMEM((chunks, per_chunk, hidden, cols), jnp.bfloat16),
            pltpu.SemaphoreType.DMA,
            pltpu.SemaphoreType.DMA((chunks,)),
            pltpu.SemaphoreType.DMA((chunks,)),
        ],
        compiler_params=pltpu.CompilerParams(vmem_limit_bytes=40 << 20),
        name="whole_grad",
    )(
        pltpu.with_memory_space_constraint(cotangent, pltpu.HBM),
        pltpu.with_memory_space_constraint(activations, pltpu.HBM),
    )


def rows_kernel(basis_hbm, out_hbm, sem):
    rows = out_hbm.shape[2]
    here = pl.multiple_of(lax.axis_index(DATA) * rows, rows)
    copies = [
        pltpu.make_async_copy(basis_hbm.at[:, pl.ds(here, rows)], out_hbm.at[i], sem.at[i])
        for i in range(out_hbm.shape[0])
    ]
    for copy in copies:
        copy.start()
    for copy in copies:
        copy.wait()


def own_rows(basis, rows):
    n = lax.axis_size("near")
    return pl.pallas_call(
        rows_kernel,
        in_specs=[pl.BlockSpec(memory_space=pltpu.HBM)],
        out_specs=pl.BlockSpec(memory_space=pltpu.HBM),
        out_shape=jax.ShapeDtypeStruct((n, basis.shape[0], rows), basis.dtype),
        scratch_shapes=[pltpu.SemaphoreType.DMA((n,))],
        name="own_rows",
    )(pltpu.with_memory_space_constraint(basis, pltpu.HBM))


def partial_kernel(pieces, basis, keep, send, partial):
    total = pieces[0].astype(jnp.float32)
    for i in range(1, pieces.shape[0]):
        total += pieces[i].astype(jnp.float32)
    high = total.astype(jnp.bfloat16)
    low = (total - high.astype(jnp.float32)).astype(jnp.bfloat16)
    over_rows = (((1,), (1,)), ((), ()))
    partial[...] = lax.dot_general(
        jnp.concatenate([basis[...], basis[...]], axis=1),
        jnp.concatenate([high, low], axis=1),
        over_rows,
        preferred_element_type=jnp.float32,
    )
    core = lax.axis_index("core")
    tiles, tile_rows = keep.shape[0], keep.shape[1]
    for tile in range(tiles):
        for ref, which in ((send, 1 - core), (keep, core)):
            first = ((tile // 2 * 2 + which) * 2 + tile % 2) * tile_rows
            ref[tile] = partial[pl.ds(pl.multiple_of(first, tile_rows), tile_rows), :].astype(
                ref.dtype
            )


def partial_grad(pieces, basis, tile_rows):
    tiles, hidden, ranks = pieces.shape[0] // 2, pieces.shape[1], basis.shape[0]
    shape = (tiles, tile_rows, hidden)
    return pl.pallas_call(
        partial_kernel,
        in_specs=[pl.BlockSpec(memory_space=pltpu.VMEM)] * 2,
        out_specs=[pl.BlockSpec(memory_space=pltpu.VMEM)] * 2,
        out_shape=[
            jax.ShapeDtypeStruct(shape, jnp.float32),
            jax.ShapeDtypeStruct(shape, jnp.bfloat16),
        ],
        scratch_shapes=[pltpu.VMEM((ranks, hidden), jnp.float32)],
        compiler_params=pltpu.CompilerParams(vmem_limit_bytes=24 << 20),
        name="partial_grad",
    )(pieces, basis)


def on_device(activations, cotangent, projection_basis, first_moment, second_moment):
    n_data = lax.axis_size(DATA)
    width, own_rank = projection_basis.shape
    rows, tile_rows, hidden = width // n_data, first_moment.shape[0], cotangent.shape[1]

    near_rows = lax.all_to_all(own_rows(projection_basis.T, rows), "near", 0, 0)
    pieces = whole_grad(cotangent.T, activations, n_data)
    pieces, near_rows = lax.optimization_barrier((pieces, near_rows))
    basis_rows = lax.all_gather(near_rows, "far", axis=0).reshape(-1, rows)

    pieces = lax.all_to_all(pieces, DATA, 0, 0)
    keep, send = partial_grad(pieces, basis_rows, tile_rows)
    sent = lax.ppermute(send, "core", ((0, 1), (1, 0)))
    tiles = lax.all_to_all((keep + sent.astype(jnp.float32)).astype(jnp.bfloat16), CHIPS, 0, 0)
    grad_tile = jnp.sum(tiles.astype(jnp.float32), axis=0)
    first_new = beta_first * first_moment + (1.0 - beta_first) * grad_tile
    second_new = beta_second * second_moment + (1.0 - beta_second) * grad_tile * grad_tile
    direction = (
        first_new / correction_first / (jnp.sqrt(second_new / correction_second) + epsilon)
    ).astype(jnp.bfloat16)
    directions = lax.all_gather(spread(direction, CHIPS), "core", axis=0)
    directions = directions.reshape(2, -1, 2, tile_rows, hidden).transpose(1, 0, 2, 3, 4)
    directions = directions.reshape(n_data * tile_rows, hidden)
    folded = lax.dot_general(
        basis_rows, directions, (((0,), (0,)), ((), ())), preferred_element_type=jnp.float32
    )
    return (galore_scale * folded, first_new, second_new)


def solution(mesh):
    dp, mp, pipe = mesh.devices.shape
    fine = Mesh(
        mesh.devices.reshape(2, dp // 4, 2, mp // 4, 4, pipe),
        ("xl", "y", "core", "far", "near", "xh"),
    )
    return jax.shard_map(
        on_device,
        mesh=fine,
        in_specs=(
            P(DATA, None),
            P(DATA, MP),
            P(None, MP),
            P(DATA, MP),
            P(DATA, MP),
        ),
        out_specs=(P(DATA, MP), P(DATA, MP), P(DATA, MP)),
        check_vma=False,
    )
```

```python
import jax
import jax.numpy as jnp
from jax import lax
from jax.experimental import pallas as pl
from jax.experimental.pallas import tpu as pltpu
from jax.sharding import Mesh, PartitionSpec as P

beta_first = 0.9
beta_second = 0.999
correction_first = 1.0
correction_second = 0.632304575
epsilon = 1e-08
galore_scale = 0.25

DATA = ("xl", "y", "core", "xh")
CHIPS = ("xl", "y", "xh")
MP = ("far", "near")


def spread(x, axes):
    n = lax.axis_size(axes)
    return lax.all_to_all(jnp.broadcast_to(x[None], (n, *x.shape)), axes, 0, 0)


def in_hbm(x):
    return pltpu.with_memory_space_constraint(x, pltpu.HBM)


def stage_kernel(basis_hbm, cot_hbm, act_hbm, rows_hbm, cot, act, sem, act_sem):
    n, _, rows = rows_hbm.shape
    here = pl.multiple_of(lax.axis_index(DATA) * rows, rows)
    copies = [
        pltpu.make_async_copy(basis_hbm.at[:, pl.ds(here, rows)], rows_hbm.at[i], sem.at[i])
        for i in range(n)
    ]
    copies.append(pltpu.make_async_copy(act_hbm.at[:, : act.shape[1]], act, act_sem.at[0]))
    copies.append(pltpu.make_async_copy(cot_hbm, cot, act_sem.at[1]))
    for copy in copies:
        copy.start()
    for copy in copies:
        copy.wait()


def stage(basis, cotangent, activations, rows):
    n, (tokens, width) = lax.axis_size("near"), activations.shape
    return pl.pallas_call(
        stage_kernel,
        in_specs=[pl.BlockSpec(memory_space=pltpu.HBM)] * 3,
        out_specs=[
            pl.BlockSpec(memory_space=pltpu.HBM),
            pl.BlockSpec(memory_space=pltpu.VMEM),
            pl.BlockSpec(memory_space=pltpu.VMEM),
        ],
        out_shape=[
            pltpu.HBM((n, basis.shape[0], rows), basis.dtype),
            pltpu.VMEM(cotangent.shape, cotangent.dtype),
            pltpu.VMEM((tokens, width // 4), activations.dtype),
        ],
        scratch_shapes=[pltpu.SemaphoreType.DMA((n,)), pltpu.SemaphoreType.DMA((2,))],
        compiler_params=pltpu.CompilerParams(vmem_limit_bytes=16 << 20),
        name="stage",
    )(in_hbm(basis), in_hbm(cotangent), in_hbm(activations))


def grad_kernel(cot, first, act_hbm, out_hbm, second, third, out, in_sem, out_sem):
    chunks, per_chunk, width = out.shape[0], out.shape[1], out.shape[3]
    cols = per_chunk * width

    def send(c):
        return pltpu.make_async_copy(
            out.at[c], out_hbm.at[c * per_chunk : (c + 1) * per_chunk], out_sem.at[c]
        )

    fetches, at = {}, first.shape[1]
    for i, act in enumerate((second, third)):
        fetches[at] = pltpu.make_async_copy(
            act_hbm.at[:, at : at + act.shape[1]], act, in_sem.at[i]
        )
        fetches[at].start()
        at += act.shape[1]
    at = 0
    for act in (first, second, third):
        if at in fetches:
            fetches[at].wait()
        for lo in range(0, act.shape[1], cols):
            block = jnp.dot(cot[...], act[:, lo : lo + cols], preferred_element_type=jnp.float32)
            c = (at + lo) // cols
            for p in range(per_chunk):
                out[c, p] = block[:, p * width : (p + 1) * width].astype(out.dtype)
            send(c).start()
        at += act.shape[1]
    for c in range(chunks):
        send(c).wait()


def whole_grad(cotangent, first, activations, pieces, chunks=8):
    hidden, (tokens, width) = cotangent.shape[0], activations.shape
    done, cols, dtype = first.shape[1], width // pieces, activations.dtype
    return pl.pallas_call(
        grad_kernel,
        in_specs=[
            pl.BlockSpec(memory_space=pltpu.VMEM),
            pl.BlockSpec(memory_space=pltpu.VMEM),
            pl.BlockSpec(memory_space=pltpu.HBM),
        ],
        out_specs=pl.BlockSpec(memory_space=pltpu.HBM),
        out_shape=pltpu.HBM((pieces, hidden, cols), jnp.bfloat16),
        scratch_shapes=[
            pltpu.VMEM((tokens, done), dtype),
            pltpu.VMEM((tokens, width - 2 * done), dtype),
            pltpu.VMEM((chunks, pieces // chunks, hidden, cols), jnp.bfloat16),
            pltpu.SemaphoreType.DMA((2,)),
            pltpu.SemaphoreType.DMA((chunks,)),
        ],
        compiler_params=pltpu.CompilerParams(vmem_limit_bytes=24 << 20),
        name="whole_grad",
    )(cotangent, first, in_hbm(activations))


def partial_kernel(pieces, basis, keep, send, partial):
    total = pieces[0].astype(jnp.float32)
    for i in range(1, pieces.shape[0]):
        total += pieces[i].astype(jnp.float32)
    high = total.astype(jnp.bfloat16)
    low = (total - high.astype(jnp.float32)).astype(jnp.bfloat16)
    over_rows = (((1,), (1,)), ((), ()))
    partial[...] = lax.dot_general(
        jnp.concatenate([basis[...], basis[...]], axis=1),
        jnp.concatenate([high, low], axis=1),
        over_rows,
        preferred_element_type=jnp.float32,
    )
    core = lax.axis_index("core")
    tiles, tile_rows = keep.shape[0], keep.shape[1]
    for tile in range(tiles):
        for ref, which in ((send, 1 - core), (keep, core)):
            first = ((tile // 2 * 2 + which) * 2 + tile % 2) * tile_rows
            ref[tile] = partial[pl.ds(pl.multiple_of(first, tile_rows), tile_rows), :].astype(
                ref.dtype
            )


def partial_grad(pieces, basis, tile_rows):
    tiles, hidden, ranks = pieces.shape[0] // 2, pieces.shape[1], basis.shape[0]
    shape = (tiles, tile_rows, hidden)
    return pl.pallas_call(
        partial_kernel,
        in_specs=[pl.BlockSpec(memory_space=pltpu.VMEM)] * 2,
        out_specs=[pl.BlockSpec(memory_space=pltpu.VMEM)] * 2,
        out_shape=[
            jax.ShapeDtypeStruct(shape, jnp.float32),
            jax.ShapeDtypeStruct(shape, jnp.bfloat16),
        ],
        scratch_shapes=[pltpu.VMEM((ranks, hidden), jnp.float32)],
        compiler_params=pltpu.CompilerParams(vmem_limit_bytes=24 << 20),
        name="partial_grad",
    )(pieces, basis)


def on_device(activations, cotangent, projection_basis, first_moment, second_moment):
    n_data = lax.axis_size(DATA)
    width, own_rank = projection_basis.shape
    rows, tile_rows, hidden = width // n_data, first_moment.shape[0], cotangent.shape[1]

    own_rows, cot, first = stage(projection_basis.T, cotangent.T, activations, rows)
    near_rows = lax.all_to_all(own_rows, "near", 0, 0)
    pieces = whole_grad(cot, first, activations, n_data)
    pieces, near_rows = lax.optimization_barrier((pieces, near_rows))
    basis_rows = lax.all_gather(near_rows, "far", axis=0).reshape(-1, rows)

    pieces = lax.all_to_all(pieces, DATA, 0, 0)
    keep, send = partial_grad(pieces, basis_rows, tile_rows)
    sent = lax.ppermute(send, "core", ((0, 1), (1, 0)))
    tiles = lax.all_to_all((keep + sent.astype(jnp.float32)).astype(jnp.bfloat16), CHIPS, 0, 0)
    grad_tile = jnp.sum(tiles.astype(jnp.float32), axis=0)
    first_new = beta_first * first_moment + (1.0 - beta_first) * grad_tile
    second_new = beta_second * second_moment + (1.0 - beta_second) * grad_tile * grad_tile
    direction = (
        first_new / correction_first / (jnp.sqrt(second_new / correction_second) + epsilon)
    ).astype(jnp.bfloat16)
    directions = lax.all_gather(spread(direction, CHIPS), "core", axis=0)
    directions = directions.reshape(2, -1, 2, tile_rows, hidden).transpose(1, 0, 2, 3, 4)
    directions = directions.reshape(n_data * tile_rows, hidden)
    folded = lax.dot_general(
        basis_rows, directions, (((0,), (0,)), ((), ())), preferred_element_type=jnp.float32
    )
    return (galore_scale * folded, first_new, second_new)


def solution(mesh):
    dp, mp, pipe = mesh.devices.shape
    fine = Mesh(
        mesh.devices.reshape(2, dp // 4, 2, mp // 4, 4, pipe),
        ("xl", "y", "core", "far", "near", "xh"),
    )
    return jax.shard_map(
        on_device,
        mesh=fine,
        in_specs=(
            P(DATA, None),
            P(DATA, MP),
            P(None, MP),
            P(DATA, MP),
            P(DATA, MP),
        ),
        out_specs=(P(DATA, MP), P(DATA, MP), P(DATA, MP)),
        check_vma=False,
    )
```

```python
import jax
import jax.numpy as jnp
from jax import lax
from jax.experimental import pallas as pl
from jax.experimental.pallas import tpu as pltpu
from jax.sharding import Mesh, PartitionSpec as P

beta_first = 0.9
beta_second = 0.999
correction_first = 1.0
correction_second = 0.632304575
epsilon = 1e-08
galore_scale = 0.25

DATA = ("xl", "y", "core", "xh")
CHIPS = ("xl", "y", "xh")
MP = ("far", "near")


def spread(x, axes):
    n = lax.axis_size(axes)
    return lax.all_to_all(jnp.broadcast_to(x[None], (n, *x.shape)), axes, 0, 0)


def in_hbm(x):
    return pltpu.with_memory_space_constraint(x, pltpu.HBM)


def stage_kernel(basis_hbm, cot_hbm, act_hbm, rows_hbm, cot, act, own, sem, in_sem):
    n, _, rows = rows_hbm.shape
    here = pl.multiple_of(lax.axis_index(DATA) * rows, rows)
    cut = pltpu.make_async_copy(basis_hbm.at[:, pl.ds(here, rows)], own, in_sem.at[0])
    cut.start()
    fetches = [
        pltpu.make_async_copy(act_hbm.at[:, : act.shape[1]], act, in_sem.at[1]),
        pltpu.make_async_copy(cot_hbm, cot, in_sem.at[2]),
    ]
    for fetch in fetches:
        fetch.start()
    cut.wait()
    copies = [pltpu.make_async_copy(own, rows_hbm.at[i], sem.at[i]) for i in range(n)]
    for copy in copies:
        copy.start()
    for copy in copies + fetches:
        copy.wait()


def stage(basis, cotangent, activations, rows):
    n, (tokens, width) = lax.axis_size("near"), activations.shape
    return pl.pallas_call(
        stage_kernel,
        in_specs=[pl.BlockSpec(memory_space=pltpu.HBM)] * 3,
        out_specs=[
            pl.BlockSpec(memory_space=pltpu.HBM),
            pl.BlockSpec(memory_space=pltpu.VMEM),
            pl.BlockSpec(memory_space=pltpu.VMEM),
        ],
        out_shape=[
            pltpu.HBM((n, basis.shape[0], rows), basis.dtype),
            pltpu.VMEM(cotangent.shape, cotangent.dtype),
            pltpu.VMEM((tokens, width // 4), activations.dtype),
        ],
        scratch_shapes=[
            pltpu.VMEM((basis.shape[0], rows), basis.dtype),
            pltpu.SemaphoreType.DMA((n,)),
            pltpu.SemaphoreType.DMA((3,)),
        ],
        compiler_params=pltpu.CompilerParams(vmem_limit_bytes=16 << 20),
        name="stage",
    )(in_hbm(basis), in_hbm(cotangent), in_hbm(activations))


def grad_kernel(cot, first, act_hbm, out_hbm, second, third, out, in_sem, out_sem):
    chunks, per_chunk, width = out.shape[0], out.shape[1], out.shape[3]
    cols = per_chunk * width

    def send(c):
        return pltpu.make_async_copy(
            out.at[c], out_hbm.at[c * per_chunk : (c + 1) * per_chunk], out_sem.at[c]
        )

    fetches, at = {}, first.shape[1]
    for i, act in enumerate((second, third)):
        fetches[at] = pltpu.make_async_copy(
            act_hbm.at[:, at : at + act.shape[1]], act, in_sem.at[i]
        )
        fetches[at].start()
        at += act.shape[1]
    at = 0
    for act in (first, second, third):
        if at in fetches:
            fetches[at].wait()
        for lo in range(0, act.shape[1], cols):
            block = jnp.dot(cot[...], act[:, lo : lo + cols], preferred_element_type=jnp.float32)
            c = (at + lo) // cols
            for p in range(per_chunk):
                out[c, p] = block[:, p * width : (p + 1) * width].astype(out.dtype)
            send(c).start()
        at += act.shape[1]
    for c in range(chunks):
        send(c).wait()


def whole_grad(cotangent, first, activations, pieces, chunks=8):
    hidden, (tokens, width) = cotangent.shape[0], activations.shape
    done, cols, dtype = first.shape[1], width // pieces, activations.dtype
    return pl.pallas_call(
        grad_kernel,
        in_specs=[
            pl.BlockSpec(memory_space=pltpu.VMEM),
            pl.BlockSpec(memory_space=pltpu.VMEM),
            pl.BlockSpec(memory_space=pltpu.HBM),
        ],
        out_specs=pl.BlockSpec(memory_space=pltpu.HBM),
        out_shape=pltpu.HBM((pieces, hidden, cols), jnp.bfloat16),
        scratch_shapes=[
            pltpu.VMEM((tokens, done), dtype),
            pltpu.VMEM((tokens, width - 2 * done), dtype),
            pltpu.VMEM((chunks, pieces // chunks, hidden, cols), jnp.bfloat16),
            pltpu.SemaphoreType.DMA((2,)),
            pltpu.SemaphoreType.DMA((chunks,)),
        ],
        compiler_params=pltpu.CompilerParams(vmem_limit_bytes=24 << 20),
        name="whole_grad",
    )(cotangent, first, in_hbm(activations))


def partial_kernel(pieces, basis, keep, send, partial):
    total = pieces[0].astype(jnp.float32)
    for i in range(1, pieces.shape[0]):
        total += pieces[i].astype(jnp.float32)
    high = total.astype(jnp.bfloat16)
    low = (total - high.astype(jnp.float32)).astype(jnp.bfloat16)
    over_rows = (((1,), (1,)), ((), ()))
    partial[...] = lax.dot_general(
        jnp.concatenate([basis[...], basis[...]], axis=1),
        jnp.concatenate([high, low], axis=1),
        over_rows,
        preferred_element_type=jnp.float32,
    )
    core = lax.axis_index("core")
    tiles, tile_rows = keep.shape[0], keep.shape[1]
    for tile in range(tiles):
        for ref, which in ((send, 1 - core), (keep, core)):
            first = ((tile // 2 * 2 + which) * 2 + tile % 2) * tile_rows
            ref[tile] = partial[pl.ds(pl.multiple_of(first, tile_rows), tile_rows), :].astype(
                ref.dtype
            )


def partial_grad(pieces, basis, tile_rows):
    tiles, hidden, ranks = pieces.shape[0] // 2, pieces.shape[1], basis.shape[0]
    shape = (tiles, tile_rows, hidden)
    return pl.pallas_call(
        partial_kernel,
        in_specs=[pl.BlockSpec(memory_space=pltpu.VMEM)] * 2,
        out_specs=[pl.BlockSpec(memory_space=pltpu.VMEM)] * 2,
        out_shape=[
            jax.ShapeDtypeStruct(shape, jnp.float32),
            jax.ShapeDtypeStruct(shape, jnp.bfloat16),
        ],
        scratch_shapes=[pltpu.VMEM((ranks, hidden), jnp.float32)],
        compiler_params=pltpu.CompilerParams(vmem_limit_bytes=24 << 20),
        name="partial_grad",
    )(pieces, basis)


def on_device(activations, cotangent, projection_basis, first_moment, second_moment):
    n_data = lax.axis_size(DATA)
    width, own_rank = projection_basis.shape
    rows, tile_rows, hidden = width // n_data, first_moment.shape[0], cotangent.shape[1]

    own_rows, cot, first = stage(projection_basis.T, cotangent.T, activations, rows)
    near_rows = lax.all_to_all(own_rows, "near", 0, 0)
    pieces = whole_grad(cot, first, activations, n_data)
    pieces, near_rows = lax.optimization_barrier((pieces, near_rows))
    basis_rows = lax.all_gather(near_rows, "far", axis=0).reshape(-1, rows)

    pieces = lax.all_to_all(pieces, DATA, 0, 0)
    keep, send = partial_grad(pieces, basis_rows, tile_rows)
    sent = lax.ppermute(send, "core", ((0, 1), (1, 0)))
    tiles = lax.all_to_all((keep + sent.astype(jnp.float32)).astype(jnp.bfloat16), CHIPS, 0, 0)
    grad_tile = jnp.sum(tiles.astype(jnp.float32), axis=0)
    first_new = beta_first * first_moment + (1.0 - beta_first) * grad_tile
    second_new = beta_second * second_moment + (1.0 - beta_second) * grad_tile * grad_tile
    direction = (
        first_new / correction_first / (jnp.sqrt(second_new / correction_second) + epsilon)
    ).astype(jnp.bfloat16)
    directions = lax.all_gather(spread(direction, CHIPS), "core", axis=0)
    directions = directions.reshape(2, -1, 2, tile_rows, hidden).transpose(1, 0, 2, 3, 4)
    directions = directions.reshape(n_data * tile_rows, hidden)
    folded = lax.dot_general(
        basis_rows, directions, (((0,), (0,)), ((), ())), preferred_element_type=jnp.float32
    )
    return (galore_scale * folded, first_new, second_new)


def solution(mesh):
    dp, mp, pipe = mesh.devices.shape
    fine = Mesh(
        mesh.devices.reshape(2, dp // 4, 2, mp // 8, 8, pipe),
        ("xl", "y", "core", "far", "near", "xh"),
    )
    return jax.shard_map(
        on_device,
        mesh=fine,
        in_specs=(
            P(DATA, None),
            P(DATA, MP),
            P(None, MP),
            P(DATA, MP),
            P(DATA, MP),
        ),
        out_specs=(P(DATA, MP), P(DATA, MP), P(DATA, MP)),
        check_vma=False,
    )
```

```python
import jax
import jax.numpy as jnp
from jax import lax
from jax.experimental import pallas as pl
from jax.experimental.pallas import tpu as pltpu
from jax.sharding import Mesh, PartitionSpec as P

beta_first = 0.9
beta_second = 0.999
correction_first = 1.0
correction_second = 0.632304575
epsilon = 1e-08
galore_scale = 0.25

DATA = ("xl", "y", "core", "xh")
CHIPS = ("xl", "y", "xh")
MP = ("far", "near")


def spread(x, axes):
    n = lax.axis_size(axes)
    return lax.all_to_all(jnp.broadcast_to(x[None], (n, *x.shape)), axes, 0, 0)


def in_hbm(x):
    return pltpu.with_memory_space_constraint(x, pltpu.HBM)


def stage_kernel(basis_hbm, cot_hbm, act_hbm, rows_hbm, cot, act, own, sem, in_sem):
    n, _, rows = rows_hbm.shape
    here = pl.multiple_of(lax.axis_index(DATA) * rows, rows)
    cut = pltpu.make_async_copy(basis_hbm.at[:, pl.ds(here, rows)], own, in_sem.at[0])
    cut.start()
    fetches = [
        pltpu.make_async_copy(act_hbm.at[:, : act.shape[1]], act, in_sem.at[1]),
        pltpu.make_async_copy(cot_hbm, cot, in_sem.at[2]),
    ]
    for fetch in fetches:
        fetch.start()
    cut.wait()
    copies = [pltpu.make_async_copy(own, rows_hbm.at[i], sem.at[i]) for i in range(n)]
    for copy in copies:
        copy.start()
    for copy in copies + fetches:
        copy.wait()


def stage(basis, cotangent, activations, rows):
    n, (tokens, width) = lax.axis_size("near"), activations.shape
    return pl.pallas_call(
        stage_kernel,
        in_specs=[pl.BlockSpec(memory_space=pltpu.HBM)] * 3,
        out_specs=[
            pl.BlockSpec(memory_space=pltpu.HBM),
            pl.BlockSpec(memory_space=pltpu.VMEM),
            pl.BlockSpec(memory_space=pltpu.VMEM),
        ],
        out_shape=[
            pltpu.HBM((n, basis.shape[0], rows), basis.dtype),
            pltpu.VMEM(cotangent.shape, cotangent.dtype),
            pltpu.VMEM((tokens, width // 4), activations.dtype),
        ],
        scratch_shapes=[
            pltpu.VMEM((basis.shape[0], rows), basis.dtype),
            pltpu.SemaphoreType.DMA((n,)),
            pltpu.SemaphoreType.DMA((3,)),
        ],
        compiler_params=pltpu.CompilerParams(vmem_limit_bytes=16 << 20),
        name="stage",
    )(in_hbm(basis), in_hbm(cotangent), in_hbm(activations))


def grad_kernel(cot, first, act_hbm, out_hbm, second, third, out, in_sem, out_sem):
    chunks, per_chunk, width = out.shape[0], out.shape[1], out.shape[3]
    cols = per_chunk * width

    def send(c):
        return pltpu.make_async_copy(
            out.at[c], out_hbm.at[c * per_chunk : (c + 1) * per_chunk], out_sem.at[c]
        )

    fetches, at = {}, first.shape[1]
    for i, act in enumerate((second, third)):
        fetches[at] = pltpu.make_async_copy(
            act_hbm.at[:, at : at + act.shape[1]], act, in_sem.at[i]
        )
        fetches[at].start()
        at += act.shape[1]
    at = 0
    for act in (first, second, third):
        if at in fetches:
            fetches[at].wait()
        for lo in range(0, act.shape[1], cols):
            block = jnp.dot(cot[...], act[:, lo : lo + cols], preferred_element_type=jnp.float32)
            c = (at + lo) // cols
            for p in range(per_chunk):
                out[c, p] = block[:, p * width : (p + 1) * width].astype(out.dtype)
            send(c).start()
        at += act.shape[1]
    for c in range(chunks):
        send(c).wait()


def whole_grad(cotangent, first, activations, pieces, chunks=8):
    hidden, (tokens, width) = cotangent.shape[0], activations.shape
    done, cols, dtype = first.shape[1], width // pieces, activations.dtype
    return pl.pallas_call(
        grad_kernel,
        in_specs=[
            pl.BlockSpec(memory_space=pltpu.VMEM),
            pl.BlockSpec(memory_space=pltpu.VMEM),
            pl.BlockSpec(memory_space=pltpu.HBM),
        ],
        out_specs=pl.BlockSpec(memory_space=pltpu.HBM),
        out_shape=pltpu.HBM((pieces, hidden, cols), jnp.bfloat16),
        scratch_shapes=[
            pltpu.VMEM((tokens, done), dtype),
            pltpu.VMEM((tokens, width - 2 * done), dtype),
            pltpu.VMEM((chunks, pieces // chunks, hidden, cols), jnp.bfloat16),
            pltpu.SemaphoreType.DMA((2,)),
            pltpu.SemaphoreType.DMA((chunks,)),
        ],
        compiler_params=pltpu.CompilerParams(vmem_limit_bytes=24 << 20),
        name="whole_grad",
    )(cotangent, first, in_hbm(activations))


def partial_kernel(pieces, basis, keep, send, partial):
    total = pieces[0].astype(jnp.float32)
    for i in range(1, pieces.shape[0]):
        total += pieces[i].astype(jnp.float32)
    high = total.astype(jnp.bfloat16)
    low = (total - high.astype(jnp.float32)).astype(jnp.bfloat16)
    over_rows = (((1,), (1,)), ((), ()))
    partial[...] = lax.dot_general(
        jnp.concatenate([basis[...], basis[...]], axis=1),
        jnp.concatenate([high, low], axis=1),
        over_rows,
        preferred_element_type=jnp.float32,
    )
    core = lax.axis_index("core")
    tiles, tile_rows = keep.shape[0], keep.shape[1]
    for tile in range(tiles):
        for ref, which in ((send, 1 - core), (keep, core)):
            first = ((tile // 2 * 2 + which) * 2 + tile % 2) * tile_rows
            ref[tile] = partial[pl.ds(pl.multiple_of(first, tile_rows), tile_rows), :].astype(
                ref.dtype
            )


def partial_grad(pieces, basis, tile_rows):
    tiles, hidden, ranks = pieces.shape[0] // 2, pieces.shape[1], basis.shape[0]
    shape = (tiles, tile_rows, hidden)
    return pl.pallas_call(
        partial_kernel,
        in_specs=[pl.BlockSpec(memory_space=pltpu.VMEM)] * 2,
        out_specs=[pl.BlockSpec(memory_space=pltpu.VMEM)] * 2,
        out_shape=[
            jax.ShapeDtypeStruct(shape, jnp.float32),
            jax.ShapeDtypeStruct(shape, jnp.bfloat16),
        ],
        scratch_shapes=[pltpu.VMEM((ranks, hidden), jnp.float32)],
        compiler_params=pltpu.CompilerParams(vmem_limit_bytes=24 << 20),
        name="partial_grad",
    )(pieces, basis)


def on_device(activations, cotangent, projection_basis, first_moment, second_moment):
    n_data = lax.axis_size(DATA)
    width, own_rank = projection_basis.shape
    rows, tile_rows, hidden = width // n_data, first_moment.shape[0], cotangent.shape[1]

    own_rows, cot, first = stage(projection_basis.T, cotangent.T, activations, rows)
    near_rows = lax.all_to_all(own_rows, "near", 0, 0)
    pieces = whole_grad(cot, first, activations, n_data)
    pieces, near_rows = lax.optimization_barrier((pieces, near_rows))
    basis_rows = lax.all_gather(near_rows, "far", axis=0).reshape(-1, rows)

    pieces = lax.all_to_all(pieces, DATA, 0, 0)
    keep, send = partial_grad(pieces, basis_rows, tile_rows)
    sent = lax.ppermute(send, "core", ((0, 1), (1, 0)))
    tiles = lax.all_to_all((keep + sent.astype(jnp.float32)).astype(jnp.bfloat16), CHIPS, 0, 0)
    grad_tile = jnp.sum(tiles.astype(jnp.float32), axis=0)
    first_new = beta_first * first_moment + (1.0 - beta_first) * grad_tile
    second_new = beta_second * second_moment + (1.0 - beta_second) * grad_tile * grad_tile
    direction = (
        first_new / correction_first / (jnp.sqrt(second_new / correction_second) + epsilon)
    ).astype(jnp.bfloat16)
    directions = lax.all_gather(spread(direction, CHIPS), "core", axis=0)
    directions = directions.reshape(2, -1, 2, tile_rows, hidden).transpose(1, 0, 2, 3, 4)
    directions = directions.reshape(n_data * tile_rows, hidden)
    folded = lax.dot_general(
        basis_rows, directions, (((0,), (0,)), ((), ())), preferred_element_type=jnp.float32
    )
    return (galore_scale * folded, first_new, second_new)


def solution(mesh):
    dp, mp, pipe = mesh.devices.shape
    fine = Mesh(
        mesh.devices.reshape(2, dp // 4, 2, mp // 4, 4, pipe),
        ("xl", "y", "core", "far", "near", "xh"),
    )
    return jax.shard_map(
        on_device,
        mesh=fine,
        in_specs=(
            P(DATA, None),
            P(DATA, MP),
            P(None, MP),
            P(DATA, MP),
            P(DATA, MP),
        ),
        out_specs=(P(DATA, MP), P(DATA, MP), P(DATA, MP)),
        check_vma=False,
    )
```

```python
import jax
import jax.numpy as jnp
from jax import lax
from jax.experimental import pallas as pl
from jax.experimental.pallas import tpu as pltpu
from jax.sharding import Mesh, PartitionSpec as P

beta_first = 0.9
beta_second = 0.999
correction_first = 1.0
correction_second = 0.632304575
epsilon = 1e-08
galore_scale = 0.25

DATA = ("xl", "y", "core", "xh")
CHIPS = ("xl", "y", "xh")
MP = ("far", "near")


def spread(x, axes):
    n = lax.axis_size(axes)
    return lax.all_to_all(jnp.broadcast_to(x[None], (n, *x.shape)), axes, 0, 0)


def in_hbm(x):
    return pltpu.with_memory_space_constraint(x, pltpu.HBM)


def stage_kernel(basis_hbm, cot_hbm, act_hbm, rows_hbm, cot, act, own, sem, in_sem):
    n, _, rows = rows_hbm.shape
    here = pl.multiple_of(lax.axis_index(DATA) * rows, rows)
    cut = pltpu.make_async_copy(basis_hbm.at[:, pl.ds(here, rows)], own, in_sem.at[0])
    cut.start()
    fetches = [
        pltpu.make_async_copy(act_hbm.at[:, : act.shape[1]], act, in_sem.at[1]),
        pltpu.make_async_copy(cot_hbm, cot, in_sem.at[2]),
    ]
    for fetch in fetches:
        fetch.start()
    cut.wait()
    copies = [pltpu.make_async_copy(own, rows_hbm.at[i], sem.at[i]) for i in range(n)]
    for copy in copies:
        copy.start()
    for copy in copies + fetches:
        copy.wait()


def stage(basis, cotangent, activations, rows):
    n, (tokens, width) = lax.axis_size("near"), activations.shape
    return pl.pallas_call(
        stage_kernel,
        in_specs=[pl.BlockSpec(memory_space=pltpu.HBM)] * 3,
        out_specs=[
            pl.BlockSpec(memory_space=pltpu.HBM),
            pl.BlockSpec(memory_space=pltpu.VMEM),
            pl.BlockSpec(memory_space=pltpu.VMEM),
        ],
        out_shape=[
            pltpu.HBM((n, basis.shape[0], rows), basis.dtype),
            pltpu.VMEM(cotangent.shape, cotangent.dtype),
            pltpu.VMEM((tokens, width // 4), activations.dtype),
        ],
        scratch_shapes=[
            pltpu.VMEM((basis.shape[0], rows), basis.dtype),
            pltpu.SemaphoreType.DMA((n,)),
            pltpu.SemaphoreType.DMA((3,)),
        ],
        compiler_params=pltpu.CompilerParams(vmem_limit_bytes=16 << 20),
        name="stage",
    )(in_hbm(basis), in_hbm(cotangent), in_hbm(activations))


def grad_kernel(cot, first, act_hbm, out_hbm, second, third, out, in_sem, out_sem):
    chunks, per_chunk, width = out.shape[0], out.shape[1], out.shape[3]
    cols = per_chunk * width

    def send(c):
        return pltpu.make_async_copy(
            out.at[c], out_hbm.at[c * per_chunk : (c + 1) * per_chunk], out_sem.at[c]
        )

    fetches, at = {}, first.shape[1]
    for i, act in enumerate((second, third)):
        fetches[at] = pltpu.make_async_copy(
            act_hbm.at[:, at : at + act.shape[1]], act, in_sem.at[i]
        )
        fetches[at].start()
        at += act.shape[1]
    at = 0
    for act in (first, second, third):
        if at in fetches:
            fetches[at].wait()
        for lo in range(0, act.shape[1], cols):
            block = jnp.dot(cot[...], act[:, lo : lo + cols], preferred_element_type=jnp.float32)
            c = (at + lo) // cols
            for p in range(per_chunk):
                out[c, p] = block[:, p * width : (p + 1) * width].astype(out.dtype)
            send(c).start()
        at += act.shape[1]
    for c in range(chunks):
        send(c).wait()


def whole_grad(cotangent, first, activations, pieces, chunks=8):
    hidden, (tokens, width) = cotangent.shape[0], activations.shape
    done, cols, dtype = first.shape[1], width // pieces, activations.dtype
    return pl.pallas_call(
        grad_kernel,
        in_specs=[
            pl.BlockSpec(memory_space=pltpu.VMEM),
            pl.BlockSpec(memory_space=pltpu.VMEM),
            pl.BlockSpec(memory_space=pltpu.HBM),
        ],
        out_specs=pl.BlockSpec(memory_space=pltpu.HBM),
        out_shape=pltpu.HBM((pieces, hidden, cols), jnp.bfloat16),
        scratch_shapes=[
            pltpu.VMEM((tokens, done), dtype),
            pltpu.VMEM((tokens, width - 2 * done), dtype),
            pltpu.VMEM((chunks, pieces // chunks, hidden, cols), jnp.bfloat16),
            pltpu.SemaphoreType.DMA((2,)),
            pltpu.SemaphoreType.DMA((chunks,)),
        ],
        compiler_params=pltpu.CompilerParams(vmem_limit_bytes=24 << 20),
        name="whole_grad",
    )(cotangent, first, in_hbm(activations))


def partial_kernel(pieces, basis, keep, send, partial):
    total = pieces[0].astype(jnp.float32)
    for i in range(1, pieces.shape[0]):
        total += pieces[i].astype(jnp.float32)
    high = total.astype(jnp.bfloat16)
    low = (total - high.astype(jnp.float32)).astype(jnp.bfloat16)
    over_rows = (((1,), (1,)), ((), ()))
    partial[...] = lax.dot_general(
        jnp.concatenate([basis[...], basis[...]], axis=1),
        jnp.concatenate([high, low], axis=1),
        over_rows,
        preferred_element_type=jnp.float32,
    )
    core = lax.axis_index("core")
    tiles, tile_rows = keep.shape[0], keep.shape[1]
    for tile in range(tiles):
        for ref, which in ((send, 1 - core), (keep, core)):
            first = ((tile // 2 * 2 + which) * 2 + tile % 2) * tile_rows
            ref[tile] = partial[pl.ds(pl.multiple_of(first, tile_rows), tile_rows), :].astype(
                ref.dtype
            )


def partial_grad(pieces, basis, tile_rows):
    tiles, hidden, ranks = pieces.shape[0] // 2, pieces.shape[1], basis.shape[0]
    shape = (tiles, tile_rows, hidden)
    return pl.pallas_call(
        partial_kernel,
        in_specs=[pl.BlockSpec(memory_space=pltpu.VMEM)] * 2,
        out_specs=[pl.BlockSpec(memory_space=pltpu.VMEM)] * 2,
        out_shape=[
            jax.ShapeDtypeStruct(shape, jnp.float32),
            jax.ShapeDtypeStruct(shape, jnp.bfloat16),
        ],
        scratch_shapes=[pltpu.VMEM((ranks, hidden), jnp.float32)],
        compiler_params=pltpu.CompilerParams(vmem_limit_bytes=24 << 20),
        name="partial_grad",
    )(pieces, basis)


def on_device(activations, cotangent, projection_basis, first_moment, second_moment):
    n_data = lax.axis_size(DATA)
    width, own_rank = projection_basis.shape
    rows, tile_rows, hidden = width // n_data, first_moment.shape[0], cotangent.shape[1]

    own_rows, cot, first = stage(projection_basis.T, cotangent.T, activations, rows)
    near_rows = lax.all_to_all(own_rows, "near", 0, 0)
    pieces = whole_grad(cot, first, activations, n_data)
    pieces, near_rows = lax.optimization_barrier((pieces, near_rows))
    chip_rows = lax.all_gather(near_rows, ("far", "core"), axis=0)
    chip_rows = chip_rows.reshape(-1, 2, *near_rows.shape)
    basis_rows = lax.dynamic_index_in_dim(chip_rows, lax.axis_index("core"), 1, keepdims=False)
    basis_rows = basis_rows.reshape(-1, rows)

    pieces = lax.all_to_all(pieces, DATA, 0, 0)
    keep, send = partial_grad(pieces, basis_rows, tile_rows)
    sent = lax.ppermute(send, "core", ((0, 1), (1, 0)))
    tiles = lax.all_to_all((keep + sent.astype(jnp.float32)).astype(jnp.bfloat16), CHIPS, 0, 0)
    grad_tile = jnp.sum(tiles.astype(jnp.float32), axis=0)
    first_new = beta_first * first_moment + (1.0 - beta_first) * grad_tile
    second_new = beta_second * second_moment + (1.0 - beta_second) * grad_tile * grad_tile
    direction = (
        first_new / correction_first / (jnp.sqrt(second_new / correction_second) + epsilon)
    ).astype(jnp.bfloat16)
    directions = lax.all_gather(spread(direction, CHIPS), "core", axis=0)
    directions = directions.reshape(2, -1, 2, tile_rows, hidden).transpose(1, 0, 2, 3, 4)
    directions = directions.reshape(n_data * tile_rows, hidden)
    folded = lax.dot_general(
        basis_rows, directions, (((0,), (0,)), ((), ())), preferred_element_type=jnp.float32
    )
    return (galore_scale * folded, first_new, second_new)


def solution(mesh):
    dp, mp, pipe = mesh.devices.shape
    fine = Mesh(
        mesh.devices.reshape(2, dp // 4, 2, mp // 4, 4, pipe),
        ("xl", "y", "core", "far", "near", "xh"),
    )
    return jax.shard_map(
        on_device,
        mesh=fine,
        in_specs=(
            P(DATA, None),
            P(DATA, MP),
            P(None, MP),
            P(DATA, MP),
            P(DATA, MP),
        ),
        out_specs=(P(DATA, MP), P(DATA, MP), P(DATA, MP)),
        check_vma=False,
    )
```

```python
import jax
import jax.numpy as jnp
from jax import lax
from jax.experimental import pallas as pl
from jax.experimental.pallas import tpu as pltpu
from jax.sharding import Mesh, PartitionSpec as P

beta_first = 0.9
beta_second = 0.999
correction_first = 1.0
correction_second = 0.632304575
epsilon = 1e-08
galore_scale = 0.25

DATA = ("xl", "y", "core", "xh")
CHIPS = ("xl", "y", "xh")
MP = ("far", "near")


def spread(x, axes):
    n = lax.axis_size(axes)
    return lax.all_to_all(jnp.broadcast_to(x[None], (n, *x.shape)), axes, 0, 0)


def in_hbm(x):
    return pltpu.with_memory_space_constraint(x, pltpu.HBM)


def stage_kernel(basis_hbm, cot_hbm, act_hbm, rows_hbm, cot, act, own, sem, in_sem):
    n, _, rows = rows_hbm.shape
    here = pl.multiple_of(lax.axis_index(DATA) * rows, rows)
    cut = pltpu.make_async_copy(basis_hbm.at[:, pl.ds(here, rows)], own, in_sem.at[0])
    cut.start()
    fetches = [
        pltpu.make_async_copy(act_hbm.at[:, : act.shape[1]], act, in_sem.at[1]),
        pltpu.make_async_copy(cot_hbm, cot, in_sem.at[2]),
    ]
    for fetch in fetches:
        fetch.start()
    cut.wait()
    copies = [pltpu.make_async_copy(own, rows_hbm.at[i], sem.at[i]) for i in range(n)]
    for copy in copies:
        copy.start()
    for copy in copies + fetches:
        copy.wait()


def stage(basis, cotangent, activations, rows):
    n, (tokens, width) = lax.axis_size("near"), activations.shape
    return pl.pallas_call(
        stage_kernel,
        in_specs=[pl.BlockSpec(memory_space=pltpu.HBM)] * 3,
        out_specs=[
            pl.BlockSpec(memory_space=pltpu.HBM),
            pl.BlockSpec(memory_space=pltpu.VMEM),
            pl.BlockSpec(memory_space=pltpu.VMEM),
        ],
        out_shape=[
            pltpu.HBM((n, basis.shape[0], rows), basis.dtype),
            pltpu.VMEM(cotangent.shape, cotangent.dtype),
            pltpu.VMEM((tokens, width // 4), activations.dtype),
        ],
        scratch_shapes=[
            pltpu.VMEM((basis.shape[0], rows), basis.dtype),
            pltpu.SemaphoreType.DMA((n,)),
            pltpu.SemaphoreType.DMA((3,)),
        ],
        compiler_params=pltpu.CompilerParams(vmem_limit_bytes=16 << 20),
        name="stage",
    )(in_hbm(basis), in_hbm(cotangent), in_hbm(activations))


def grad_kernel(
    cot, first, act_hbm, keep_hbm, send_hbm, second, third, out, in_sem, out_sem
):
    chunks, per_chunk, width = out.shape[0], out.shape[1], out.shape[3]
    cols, half = per_chunk * width, per_chunk // 2
    core = lax.axis_index("core")

    def copy(c, which, to):
        return pltpu.make_async_copy(
            out.at[c, which * half : (which + 1) * half],
            to.at[c * half : (c + 1) * half],
            out_sem.at[c, which],
        )

    def send(c):
        @pl.when(core == 0)
        def _():
            copy(c, 0, keep_hbm).start()
            copy(c, 1, send_hbm).start()

        @pl.when(core == 1)
        def _():
            copy(c, 0, send_hbm).start()
            copy(c, 1, keep_hbm).start()

    fetches, at = {}, first.shape[1]
    for i, act in enumerate((second, third)):
        fetches[at] = pltpu.make_async_copy(
            act_hbm.at[:, at : at + act.shape[1]], act, in_sem.at[i]
        )
        fetches[at].start()
        at += act.shape[1]
    at = 0
    for act in (first, second, third):
        if at in fetches:
            fetches[at].wait()
        for lo in range(0, act.shape[1], cols):
            block = jnp.dot(cot[...], act[:, lo : lo + cols], preferred_element_type=jnp.float32)
            c = (at + lo) // cols
            for p in range(per_chunk):
                out[c, p] = block[:, p * width : (p + 1) * width].astype(out.dtype)
            send(c)
        at += act.shape[1]

    @pl.when(core == 0)
    def _():
        for c in range(chunks):
            copy(c, 0, keep_hbm).wait()
            copy(c, 1, send_hbm).wait()

    @pl.when(core == 1)
    def _():
        for c in range(chunks):
            copy(c, 0, send_hbm).wait()
            copy(c, 1, keep_hbm).wait()


def whole_grad(cotangent, first, activations, pieces):
    hidden, (tokens, width) = cotangent.shape[0], activations.shape
    done, cols, dtype = first.shape[1], width // pieces, activations.dtype
    chunks, per_chunk = pieces // 4, 4
    return pl.pallas_call(
        grad_kernel,
        in_specs=[
            pl.BlockSpec(memory_space=pltpu.VMEM),
            pl.BlockSpec(memory_space=pltpu.VMEM),
            pl.BlockSpec(memory_space=pltpu.HBM),
        ],
        out_specs=[pl.BlockSpec(memory_space=pltpu.HBM)] * 2,
        out_shape=[pltpu.HBM((pieces // 2, hidden, cols), jnp.bfloat16)] * 2,
        scratch_shapes=[
            pltpu.VMEM((tokens, done), dtype),
            pltpu.VMEM((tokens, width - 2 * done), dtype),
            pltpu.VMEM((chunks, per_chunk, hidden, cols), jnp.bfloat16),
            pltpu.SemaphoreType.DMA((2,)),
            pltpu.SemaphoreType.DMA((chunks, 2)),
        ],
        compiler_params=pltpu.CompilerParams(vmem_limit_bytes=24 << 20),
        name="whole_grad",
    )(cotangent, first, in_hbm(activations))


def with_other_core(keep, send):
    sent = lax.ppermute(send, "core", ((0, 1), (1, 0)))
    return (keep.astype(jnp.float32) + sent.astype(jnp.float32)).astype(jnp.bfloat16)


def partial_kernel(pieces, basis, keep, send, partial):
    total = pieces[0].astype(jnp.float32)
    for i in range(1, pieces.shape[0]):
        total += pieces[i].astype(jnp.float32)
    high = total.astype(jnp.bfloat16)
    low = (total - high.astype(jnp.float32)).astype(jnp.bfloat16)
    over_rows = (((1,), (1,)), ((), ()))
    partial[...] = lax.dot_general(
        jnp.concatenate([basis[...], basis[...]], axis=1),
        jnp.concatenate([high, low], axis=1),
        over_rows,
        preferred_element_type=jnp.float32,
    )
    core = lax.axis_index("core")
    tiles, tile_rows = keep.shape[0], keep.shape[1]
    for tile in range(tiles):
        for ref, which in ((send, 1 - core), (keep, core)):
            first = ((tile // 2 * 2 + which) * 2 + tile % 2) * tile_rows
            ref[tile] = partial[pl.ds(pl.multiple_of(first, tile_rows), tile_rows), :].astype(
                ref.dtype
            )


def partial_grad(pieces, basis, tile_rows):
    tiles, hidden, ranks = pieces.shape[0], pieces.shape[1], basis.shape[0]
    shape = (tiles, tile_rows, hidden)
    return pl.pallas_call(
        partial_kernel,
        in_specs=[pl.BlockSpec(memory_space=pltpu.VMEM)] * 2,
        out_specs=[pl.BlockSpec(memory_space=pltpu.VMEM)] * 2,
        out_shape=[
            jax.ShapeDtypeStruct(shape, jnp.float32),
            jax.ShapeDtypeStruct(shape, jnp.bfloat16),
        ],
        scratch_shapes=[pltpu.VMEM((ranks, hidden), jnp.float32)],
        compiler_params=pltpu.CompilerParams(vmem_limit_bytes=24 << 20),
        name="partial_grad",
    )(pieces, basis)


def on_device(activations, cotangent, projection_basis, first_moment, second_moment):
    n_data = lax.axis_size(DATA)
    width, own_rank = projection_basis.shape
    rows, tile_rows, hidden = width // n_data, first_moment.shape[0], cotangent.shape[1]

    own_rows, cot, first = stage(projection_basis.T, cotangent.T, activations, rows)
    near_rows = lax.all_to_all(own_rows, "near", 0, 0)
    keep, send = whole_grad(cot, first, activations, n_data)
    keep, send, near_rows = lax.optimization_barrier((keep, send, near_rows))
    pieces = with_other_core(keep, send)
    pieces, near_rows = lax.optimization_barrier((pieces, near_rows))
    chip_rows = lax.all_gather(near_rows, ("far", "core"), axis=0)
    chip_rows = chip_rows.reshape(-1, 2, *near_rows.shape)
    basis_rows = lax.dynamic_index_in_dim(chip_rows, lax.axis_index("core"), 1, keepdims=False)
    basis_rows = basis_rows.reshape(-1, rows)

    pieces = lax.all_to_all(pieces, CHIPS, 0, 0)
    keep, send = partial_grad(pieces, basis_rows, tile_rows)
    tiles = lax.all_to_all(with_other_core(keep, send), CHIPS, 0, 0)
    grad_tile = jnp.sum(tiles.astype(jnp.float32), axis=0)
    first_new = beta_first * first_moment + (1.0 - beta_first) * grad_tile
    second_new = beta_second * second_moment + (1.0 - beta_second) * grad_tile * grad_tile
    direction = (
        first_new / correction_first / (jnp.sqrt(second_new / correction_second) + epsilon)
    ).astype(jnp.bfloat16)
    directions = lax.all_gather(spread(direction, CHIPS), "core", axis=0)
    directions = directions.reshape(2, -1, 2, tile_rows, hidden).transpose(1, 0, 2, 3, 4)
    directions = directions.reshape(n_data * tile_rows, hidden)
    folded = lax.dot_general(
        basis_rows, directions, (((0,), (0,)), ((), ())), preferred_element_type=jnp.float32
    )
    return (galore_scale * folded, first_new, second_new)


def solution(mesh):
    dp, mp, pipe = mesh.devices.shape
    fine = Mesh(
        mesh.devices.reshape(2, dp // 4, 2, mp // 4, 4, pipe),
        ("xl", "y", "core", "far", "near", "xh"),
    )
    return jax.shard_map(
        on_device,
        mesh=fine,
        in_specs=(
            P(DATA, None),
            P(DATA, MP),
            P(None, MP),
            P(DATA, MP),
            P(DATA, MP),
        ),
        out_specs=(P(DATA, MP), P(DATA, MP), P(DATA, MP)),
        check_vma=False,
    )
```

```python
import jax
import jax.numpy as jnp
from jax import lax
from jax.experimental import pallas as pl
from jax.experimental.pallas import tpu as pltpu
from jax.sharding import Mesh, PartitionSpec as P

beta_first = 0.9
beta_second = 0.999
correction_first = 1.0
correction_second = 0.632304575
epsilon = 1e-08
galore_scale = 0.25

DATA = ("xl", "y", "core", "xh")
CHIPS = ("xl", "y", "xh")
MP = ("far", "near")


def spread(x, axes):
    n = lax.axis_size(axes)
    return lax.all_to_all(jnp.broadcast_to(x[None], (n, *x.shape)), axes, 0, 0)


def in_hbm(x):
    return pltpu.with_memory_space_constraint(x, pltpu.HBM)


def stage_kernel(basis_hbm, cot_hbm, act_hbm, rows_hbm, cot, act, own, sem, in_sem):
    n, _, rows = rows_hbm.shape
    here = pl.multiple_of(lax.axis_index(DATA) * rows, rows)
    cut = pltpu.make_async_copy(basis_hbm.at[:, pl.ds(here, rows)], own, in_sem.at[0])
    cut.start()
    fetches = [
        pltpu.make_async_copy(act_hbm.at[:, : act.shape[1]], act, in_sem.at[1]),
        pltpu.make_async_copy(cot_hbm, cot, in_sem.at[2]),
    ]
    for fetch in fetches:
        fetch.start()
    cut.wait()
    copies = [pltpu.make_async_copy(own, rows_hbm.at[i], sem.at[i]) for i in range(n)]
    for copy in copies:
        copy.start()
    for copy in copies + fetches:
        copy.wait()


def stage(basis, cotangent, activations, rows):
    n, (tokens, width) = lax.axis_size("near"), activations.shape
    return pl.pallas_call(
        stage_kernel,
        in_specs=[pl.BlockSpec(memory_space=pltpu.HBM)] * 3,
        out_specs=[
            pl.BlockSpec(memory_space=pltpu.HBM),
            pl.BlockSpec(memory_space=pltpu.VMEM),
            pl.BlockSpec(memory_space=pltpu.VMEM),
        ],
        out_shape=[
            pltpu.HBM((n, basis.shape[0], rows), basis.dtype),
            pltpu.VMEM(cotangent.shape, cotangent.dtype),
            pltpu.VMEM((tokens, width // 4), activations.dtype),
        ],
        scratch_shapes=[
            pltpu.VMEM((basis.shape[0], rows), basis.dtype),
            pltpu.SemaphoreType.DMA((n,)),
            pltpu.SemaphoreType.DMA((3,)),
        ],
        compiler_params=pltpu.CompilerParams(vmem_limit_bytes=16 << 20),
        name="stage",
    )(in_hbm(basis), in_hbm(cotangent), in_hbm(activations))


def grad_kernel(cot, first, act_hbm, out_hbm, second, third, out, in_sem, out_sem):
    chunks, per_chunk, width = out.shape[0], out.shape[1], out.shape[3]
    cols = per_chunk * width

    def send(c):
        return pltpu.make_async_copy(
            out.at[c], out_hbm.at[c * per_chunk : (c + 1) * per_chunk], out_sem.at[c]
        )

    fetches, at = {}, first.shape[1]
    for i, act in enumerate((second, third)):
        fetches[at] = pltpu.make_async_copy(
            act_hbm.at[:, at : at + act.shape[1]], act, in_sem.at[i]
        )
        fetches[at].start()
        at += act.shape[1]
    at = 0
    for act in (first, second, third):
        if at in fetches:
            fetches[at].wait()
        for lo in range(0, act.shape[1], cols):
            block = jnp.dot(cot[...], act[:, lo : lo + cols], preferred_element_type=jnp.float32)
            c = (at + lo) // cols
            for p in range(per_chunk):
                out[c, p] = block[:, p * width : (p + 1) * width].astype(out.dtype)
            send(c).start()
        at += act.shape[1]
    for c in range(chunks):
        send(c).wait()


def whole_grad(cotangent, first, activations, pieces, chunks=8):
    hidden, (tokens, width) = cotangent.shape[0], activations.shape
    done, cols, dtype = first.shape[1], width // pieces, activations.dtype
    return pl.pallas_call(
        grad_kernel,
        in_specs=[
            pl.BlockSpec(memory_space=pltpu.VMEM),
            pl.BlockSpec(memory_space=pltpu.VMEM),
            pl.BlockSpec(memory_space=pltpu.HBM),
        ],
        out_specs=pl.BlockSpec(memory_space=pltpu.HBM),
        out_shape=pltpu.HBM((pieces, hidden, cols), jnp.bfloat16),
        scratch_shapes=[
            pltpu.VMEM((tokens, done), dtype),
            pltpu.VMEM((tokens, width - 2 * done), dtype),
            pltpu.VMEM((chunks, pieces // chunks, hidden, cols), jnp.bfloat16),
            pltpu.SemaphoreType.DMA((2,)),
            pltpu.SemaphoreType.DMA((chunks,)),
        ],
        compiler_params=pltpu.CompilerParams(vmem_limit_bytes=24 << 20),
        name="whole_grad",
    )(cotangent, first, in_hbm(activations))


def partial_kernel(pieces, basis, keep, send, partial):
    total = pieces[0].astype(jnp.float32)
    for i in range(1, pieces.shape[0]):
        total += pieces[i].astype(jnp.float32)
    high = total.astype(jnp.bfloat16)
    low = (total - high.astype(jnp.float32)).astype(jnp.bfloat16)
    over_rows = (((1,), (1,)), ((), ()))
    partial[...] = lax.dot_general(
        jnp.concatenate([basis[...], basis[...]], axis=1),
        jnp.concatenate([high, low], axis=1),
        over_rows,
        preferred_element_type=jnp.float32,
    )
    core = lax.axis_index("core")
    tiles, tile_rows = keep.shape[0], keep.shape[1]
    for tile in range(tiles):
        for ref, which in ((send, 1 - core), (keep, core)):
            first = ((tile // 2 * 2 + which) * 2 + tile % 2) * tile_rows
            ref[tile] = partial[pl.ds(pl.multiple_of(first, tile_rows), tile_rows), :].astype(
                ref.dtype
            )


def partial_grad(pieces, basis, tile_rows):
    tiles, hidden, ranks = pieces.shape[0] // 2, pieces.shape[1], basis.shape[0]
    shape = (tiles, tile_rows, hidden)
    return pl.pallas_call(
        partial_kernel,
        in_specs=[pl.BlockSpec(memory_space=pltpu.VMEM)] * 2,
        out_specs=[pl.BlockSpec(memory_space=pltpu.VMEM)] * 2,
        out_shape=[
            jax.ShapeDtypeStruct(shape, jnp.float32),
            jax.ShapeDtypeStruct(shape, jnp.bfloat16),
        ],
        scratch_shapes=[pltpu.VMEM((ranks, hidden), jnp.float32)],
        compiler_params=pltpu.CompilerParams(vmem_limit_bytes=24 << 20),
        name="partial_grad",
    )(pieces, basis)


def on_device(activations, cotangent, projection_basis, first_moment, second_moment):
    n_data = lax.axis_size(DATA)
    width, own_rank = projection_basis.shape
    rows, tile_rows, hidden = width // n_data, first_moment.shape[0], cotangent.shape[1]

    own_rows, cot, first = stage(projection_basis.T, cotangent.T, activations, rows)
    near_rows = lax.all_to_all(own_rows, "near", 0, 0)
    pieces = whole_grad(cot, first, activations, n_data)
    pieces, near_rows = lax.optimization_barrier((pieces, near_rows))
    chip_rows = lax.all_gather(near_rows, ("far", "core"), axis=0)
    chip_rows = chip_rows.reshape(-1, 2, *near_rows.shape)
    basis_rows = lax.dynamic_index_in_dim(chip_rows, lax.axis_index("core"), 1, keepdims=False)
    basis_rows = basis_rows.reshape(-1, rows)

    pieces = lax.all_to_all(pieces, DATA, 0, 0)
    keep, send = partial_grad(pieces, basis_rows, tile_rows)
    sent = lax.ppermute(send, "core", ((0, 1), (1, 0)))
    tiles = lax.all_to_all((keep + sent.astype(jnp.float32)).astype(jnp.bfloat16), CHIPS, 0, 0)
    grad_tile = jnp.sum(tiles.astype(jnp.float32), axis=0)
    first_new = beta_first * first_moment + (1.0 - beta_first) * grad_tile
    second_new = beta_second * second_moment + (1.0 - beta_second) * grad_tile * grad_tile
    direction = (
        first_new / correction_first / (jnp.sqrt(second_new / correction_second) + epsilon)
    ).astype(jnp.bfloat16)
    directions = lax.all_gather(spread(direction, CHIPS), "core", axis=0)
    directions = directions.reshape(2, -1, 2, tile_rows, hidden).transpose(1, 0, 2, 3, 4)
    directions = directions.reshape(n_data * tile_rows, hidden)
    folded = lax.dot_general(
        basis_rows, directions, (((0,), (0,)), ((), ())), preferred_element_type=jnp.float32
    )
    return (galore_scale * folded, first_new, second_new)


def solution(mesh):
    dp, mp, pipe = mesh.devices.shape
    fine = Mesh(
        mesh.devices.reshape(2, dp // 4, 2, mp // 2, 2, pipe),
        ("xl", "y", "core", "far", "near", "xh"),
    )
    return jax.shard_map(
        on_device,
        mesh=fine,
        in_specs=(
            P(DATA, None),
            P(DATA, MP),
            P(None, MP),
            P(DATA, MP),
            P(DATA, MP),
        ),
        out_specs=(P(DATA, MP), P(DATA, MP), P(DATA, MP)),
        check_vma=False,
    )
```
